32 devices in a mesh: groups: 2 (over y), site: 4 (over z), member: 4 (over x, core).
Axes of the slice: x: 2, y: 2, z: 4, core: 2. Of those that a mesh axis runs over, the one named last changes fastest.
Arguments:
- tokens: bfloat16 [2048, 2880], P(('groups', 'site', 'member')), parts along dimension 0, may hold values from -6 to 6
- expert_ids: int32 [2048, 4], P(('groups', 'site', 'member')), parts along dimension 0, may hold values from 0 to 15, as said below
- route_weights: bfloat16 [2048, 4], P(('groups', 'site', 'member')), parts along dimension 0, may hold values from 0.049804688 to 1
- w_gate: bfloat16 [16, 2880, 2880], P(('site', 'member')), may hold values from -0.109375 to 0.109375
- w_up: bfloat16 [16, 2880, 2880], P(('site', 'member')), may hold values from -0.109375 to 0.109375
- w_down: bfloat16 [16, 2880, 2880], P(('site', 'member')), may hold values from -0.109375 to 0.109375
Outputs:
- mixed: bfloat16 [2048, 2880], P(('groups', 'site', 'member')), parts along dimension 0
The draws below stay inside these ranges and needn't reach their ends.
There are 2 independent parts, one for each index of `groups`. The reference program is written for one: setup_inputs(seed, part) draws one part's arguments, and reference() takes and returns one part's arrays. A program takes and returns all parts, laid end to end along the dimension named above; an argument that names none is the same for every part. Nothing has to cross between parts.
Inputs may be any that keep to these rules, and one draw needn't show every extreme that they name: `expert_ids`: each row names 4 different experts. At most 18 of the 64 tokens of one device name any one expert.
All inputs are finite; a program needn't handle non-finite values.
Results may differ from the reference program's by a relative error of at most 0.014.
Values may be sent and summed in bfloat16 or wider, within the bound.
No kernel may reach another device: no remote copies, remote signals or barrier semaphores. Data moves between devices by JAX's collectives and lax.ppermute only.
A program may use at most 192 MiB of HBM per device.

```python
import math
import jax
import jax.numpy as jnp
import numpy as np
from jax import lax

D = 2880
FF = 2880
TOP = 4
TOK_DEV = 64
EXP_SITE = 4
EXPERTS = 16
SPLIT = 1
FFS = 2880
TOKENS = 1024
MOST = 18
N_SITE = 4
N_MEMBER = 4


def draw_expert_ids(key, part):
    device_total = N_SITE * N_MEMBER
    expert_total = EXP_SITE * N_SITE
    mean_load = TOK_DEV * TOP // expert_total
    spread = MOST - mean_load
    pair_total = expert_total // 2
    rest_pairs = pair_total - EXP_SITE
    first_table = np.concatenate([np.arange(EXP_SITE), 2 * EXP_SITE + 2 * np.arange(rest_pairs)]).astype(np.int32)
    second_table = np.concatenate([EXP_SITE + np.arange(EXP_SITE), 2 * EXP_SITE + 2 * np.arange(rest_pairs) + 1]).astype(np.int32)
    pair_first = jnp.asarray(first_table, jnp.int32)
    pair_second = jnp.asarray(second_table, jnp.int32)
    hot_expert = jax.random.randint(jax.random.fold_in(key, 11), (), 0, expert_total)
    hot_member = jax.random.randint(jax.random.fold_in(key, 12), (), 0, N_MEMBER)
    hot_site = hot_expert // EXP_SITE
    site_first = hot_site * EXP_SITE + (hot_expert % EXP_SITE + jnp.arange(EXP_SITE, dtype=jnp.int32)) % EXP_SITE
    pair_ids = jnp.arange(pair_total, dtype=jnp.int32)

    def device_ids(device):
        device_key = jax.random.fold_in(jax.random.fold_in(key, 13), device)
        key_order, key_delta, key_perm, key_roll = jax.random.split(device_key, 4)
        others_rank = jax.random.permutation(key_order, expert_total - EXP_SITE).astype(jnp.int32)
        others = jnp.where(others_rank >= hot_site * EXP_SITE, others_rank + EXP_SITE, others_rank)
        expert_order = jnp.concatenate([site_first.astype(jnp.int32), others.astype(jnp.int32)])
        deltas = jax.random.randint(key_delta, (pair_total,), -spread, spread + 1)
        forced = (pair_ids == 0) | (device % N_MEMBER == hot_member) & (pair_ids < EXP_SITE)
        deltas = jnp.where(forced, spread, deltas)
        counts = jnp.zeros((expert_total,), jnp.int32).at[pair_first].set(mean_load + deltas).at[pair_second].set(mean_load - deltas)
        tickets = jnp.repeat(expert_order, counts, total_repeat_length=TOK_DEV * TOP)
        layout = tickets.reshape(TOP, TOK_DEV).T
        permuted = layout[jax.random.permutation(key_perm, TOK_DEV)]
        shifts = jax.random.randint(key_roll, (TOK_DEV, 1), 0, TOP)
        columns = (jnp.arange(TOP, dtype=jnp.int32)[None, :] + shifts) % TOP
        return jnp.take_along_axis(permuted, columns, axis=1)
    all_devices = jax.vmap(device_ids)(jnp.arange(device_total, dtype=jnp.int32))
    return all_devices.reshape(device_total * TOK_DEV, TOP).astype(jnp.int32)


def levels(own_key, extent, pieces, low, top_value):
    loudness, own = 1.0, jax.random.fold_in(own_key, 6)
    for axis_at, shards_of in pieces:
        steps = jnp.exp(jax.random.uniform(jax.random.fold_in(own, axis_at), (shards_of,), jnp.float32, low / len(pieces), top_value / len(pieces)))
        loudness = loudness * jnp.repeat(steps, extent[axis_at] // shards_of).reshape([-1 if axis == axis_at else 1 for axis in range(len(extent))])
    return loudness


def scatter_about(stream_key, dims, width, reach, shards=(), kind=jnp.bfloat16):
    values = width * jax.random.normal(stream_key, dims, jnp.float32)
    if shards:
        values = values * levels(stream_key, dims, shards, -0.22, 0.18)
    return jnp.clip(values, -reach, reach).astype(kind)


def setup_inputs(seed: int = 0, part: int = 0) -> dict:
    seeds = jax.random.split(jax.random.key(seed), 7)
    own_keys = jax.random.split(jax.random.fold_in(seeds[6], part), 7)
    tokens = scatter_about(own_keys[0], (TOKENS, D), 1.0, 6.0, ((0, 16),))
    expert_ids = draw_expert_ids(jax.random.fold_in(jax.random.fold_in(seeds[6], part), 71), part)
    route_weights = jnp.clip(jnp.exp(math.log(1.0) - 2.9996462 * jax.random.uniform(own_keys[2], (TOKENS, TOP), jnp.float32) ** levels(own_keys[2], (TOKENS, TOP), ((0, 16),), -0.2, 0.2)), 0.049804688, 1.0).astype(jnp.bfloat16)
    w_gate = scatter_about(seeds[3], (EXPERTS * SPLIT, D, FFS), D ** -0.5, 0.109375, ((0, 16),))
    w_up = scatter_about(seeds[4], (EXPERTS * SPLIT, D, FFS), D ** -0.5, 0.109375, ((0, 16),))
    w_down = scatter_about(seeds[5], (EXPERTS * SPLIT, FFS, D), FF ** -0.5, 0.109375, ((0, 16),))
    return dict(tokens=tokens, expert_ids=expert_ids, route_weights=route_weights, w_gate=w_gate, w_up=w_up, w_down=w_down)


alpha_glu = 1.702


def expert_partial(inputs, gate_weight, up_weight, down_weight):
    gate_value = jnp.dot(inputs, gate_weight, preferred_element_type=jnp.float32)
    up_value = jnp.dot(inputs, up_weight, preferred_element_type=jnp.float32)
    hidden = ((up_value + 1.0) * gate_value * jax.nn.sigmoid(alpha_glu * gate_value)).astype(jnp.bfloat16)
    return jnp.dot(hidden, down_weight, preferred_element_type=jnp.float32).astype(jnp.bfloat16)


def reference(tokens, expert_ids, route_weights, w_gate, w_up, w_down):
    count_tokens = tokens.shape[0]
    top_count = expert_ids.shape[1]
    split_count = N_MEMBER // EXP_SITE
    capacity = N_SITE * N_MEMBER * MOST
    flat_ids = expert_ids.reshape(-1)
    flat_weight = route_weights.reshape(-1).astype(jnp.float32)
    flat_token = jnp.arange(count_tokens * top_count, dtype=jnp.int32) // top_count

    def one_site(running_sum, site_number):
        site_total = jnp.zeros(tokens.shape, jnp.float32)
        for within in range(EXP_SITE):
            expert = site_number * EXP_SITE + within
            chosen = flat_ids == expert
            position = jnp.cumsum(chosen.astype(jnp.int32)) - 1
            target = jnp.where(chosen, position, capacity).astype(jnp.int32)
            row_ids = jnp.zeros((capacity,), jnp.int32).at[target].set(flat_token, mode="drop")
            row_weight = jnp.zeros((capacity,), jnp.float32).at[target].set(flat_weight, mode="drop")
            inputs = tokens[row_ids]
            summed = jnp.zeros((capacity, tokens.shape[1]), jnp.float32)
            for shard_index in range(split_count):
                weight_index = expert * split_count + shard_index
                partial_out = expert_partial(inputs, w_gate[weight_index], w_up[weight_index], w_down[weight_index])
                summed = summed + partial_out.astype(jnp.float32)
            site_total = site_total.at[row_ids].add(row_weight[:, None] * summed)
        rounded = lax.optimization_barrier(site_total.astype(jnp.bfloat16))
        return running_sum + rounded.astype(jnp.float32), site_number

    start_sum = jnp.zeros(tokens.shape, jnp.float32)
    running_sum, unused = lax.scan(one_site, start_sum, jnp.arange(N_SITE, dtype=jnp.int32))
    return running_sum.astype(jnp.bfloat16)
```

```python
import functools

import jax
import jax.numpy as jnp
from jax import lax
from jax.experimental import pallas as pl
from jax.experimental.pallas import tpu as pltpu
from jax.sharding import PartitionSpec as P

EXP_SITE = 4
LANE = 128
SUB = 8
TILE = 512

alpha_glu = 1.702


class Fold:
    def __init__(self, rows, width):
        self.rows = rows
        self.width = width
        self.padded = -(-width // LANE) * LANE
        self.groups = rows // SUB
        self.rest = rows % SUB
        if self.rest and SUB % self.rest:
            self.groups, self.rest = self.groups + 1, 0
        self.pieces = SUB // self.rest if self.rest else 0
        tiles = self.padded // LANE
        self.piece = -(-tiles // self.pieces) * LANE if self.rest else 0
        self.tail_at = self.groups * self.padded
        self.total = self.tail_at + self.piece
        self.slots = self.groups * SUB + self.rest

    def spans(self):
        for p in range(self.pieces):
            lo = p * self.piece
            hi = min(self.width, lo + self.piece)
            if hi > lo:
                yield p, lo, hi


def slot_masks(route, fold, chunks):
    half = route.shape[0] // 2
    tokens = route.shape[1]
    shape = (chunks * SUB, tokens)
    row = lax.broadcasted_iota(jnp.int32, shape, 0)
    group = (row // SUB).astype(jnp.float32)
    sub = row % SUB
    need = jnp.zeros(shape, jnp.float32)
    weight = jnp.zeros(shape, jnp.float32)
    for k in range(half):
        hit = route[k : k + 1, :] == group
        need = jnp.where(hit, 1.0, need)
        weight = jnp.where(hit, route[half + k : half + k + 1, :], weight)
    before = (
        lax.broadcasted_iota(jnp.int32, (tokens, tokens), 0)
        < lax.broadcasted_iota(jnp.int32, (tokens, tokens), 1)
    ).astype(jnp.bfloat16)
    position = jnp.dot(need.astype(jnp.bfloat16), before, preferred_element_type=jnp.float32)
    position = jnp.where(need > 0, position, -1.0)
    subf = sub.astype(jnp.float32)
    mains = [position == subf + float(SUB * q) for q in range(fold.groups)]
    tails = []
    for p in range(fold.pieces):
        slot = (sub // fold.pieces).astype(jnp.float32) + float(SUB * fold.groups)
        tails.append((position == slot) & (sub % fold.pieces == p))
    return mains, tails, weight


def pack_kernel(fold, chunks, route_ref, tokens_ref, out_ref):
    mains, tails, _ = slot_masks(route_ref[...], fold, chunks)
    for q, mask in enumerate(mains):
        pick = jnp.where(mask, 1.0, 0.0).astype(jnp.bfloat16)
        rows = jnp.dot(pick, tokens_ref[...], preferred_element_type=jnp.float32)
        lo = q * fold.padded
        out_ref[:, lo : lo + fold.width] = rows.astype(jnp.bfloat16)
    if tails:
        total = None
        for p, lo, hi in fold.spans():
            pick = jnp.where(tails[p], 1.0, 0.0).astype(jnp.bfloat16)
            piece = jnp.dot(pick, tokens_ref[:, lo:hi], preferred_element_type=jnp.float32)
            if hi - lo < fold.piece:
                blank = jnp.zeros((piece.shape[0], fold.piece - (hi - lo)), jnp.float32)
                piece = jnp.concatenate([piece, blank], axis=1)
            total = piece if total is None else total + piece
        out_ref[:, fold.tail_at :] = total.astype(jnp.bfloat16)


def weighted_sum(fold, chunks, route, returned_ref):
    mains, tails, weight = slot_masks(route, fold, chunks)
    contract = (((0,), (0,)), ((), ()))
    total = None
    for q, mask in enumerate(mains):
        scale = jnp.where(mask, weight, 0.0).astype(jnp.bfloat16)
        lo = q * fold.padded
        term = lax.dot_general(
            scale,
            returned_ref[:, lo : lo + fold.width],
            contract,
            preferred_element_type=jnp.float32,
        )
        total = term if total is None else total + term
    if tails:
        pieces = []
        for p, lo, hi in fold.spans():
            scale = jnp.where(tails[p], weight, 0.0).astype(jnp.bfloat16)
            pieces.append(
                lax.dot_general(
                    scale,
                    returned_ref[:, fold.tail_at : fold.tail_at + (hi - lo)],
                    contract,
                    preferred_element_type=jnp.float32,
                )
            )
        term = jnp.concatenate(pieces, axis=1)
        total = term if total is None else total + term
    return total


def held_kernel(fold, chunks, route_ref, returned_ref, out_ref):
    out_ref[...] = weighted_sum(fold, chunks, route_ref[...], returned_ref).astype(jnp.bfloat16)


def final_kernel(fold, chunks, route_ref, returned_ref, other_ref, out_ref):
    total = weighted_sum(fold, chunks, route_ref[...], returned_ref)
    out_ref[...] = (total + other_ref[...].astype(jnp.float32)).astype(jnp.bfloat16)


def tail_pick(fold, sources, p):
    shape = (sources * fold.rest, sources * SUB)
    row = lax.broadcasted_iota(jnp.int32, shape, 0)
    col = lax.broadcasted_iota(jnp.int32, shape, 1)
    want = (row // fold.rest) * SUB + (row % fold.rest) * fold.pieces + p
    return jnp.where(col == want, 1.0, 0.0).astype(jnp.bfloat16)


def expert_kernel(
    fold, sources, up_steps, own_ref, far_ref, gate_ref, up_ref, down_ref,
    own_out, far_out, x_ref, h_ref, o_ref,
):
    step = pl.program_id(0)
    width = fold.width
    ff = h_ref.shape[1]
    part = sources * fold.slots
    block = sources * SUB

    @pl.when(step == 0)
    def _():
        for base, src in ((0, own_ref), (part, far_ref)):
            for q in range(fold.groups):
                lo = q * fold.padded
                x_ref[base + q * block : base + (q + 1) * block, :] = src[:, lo : lo + width]
            at = base + fold.groups * block
            for p, lo, hi in fold.spans():
                rows = jnp.dot(
                    tail_pick(fold, sources, p),
                    src[:, fold.tail_at : fold.tail_at + (hi - lo)],
                    preferred_element_type=jnp.float32,
                )
                x_ref[at : at + sources * fold.rest, lo:hi] = rows.astype(jnp.bfloat16)

    @pl.when(step < up_steps)
    def _():
        gate = jnp.dot(x_ref[...], gate_ref[0], preferred_element_type=jnp.float32)
        up = jnp.dot(x_ref[...], up_ref[0], preferred_element_type=jnp.float32)
        hidden = ((up + 1.0) * gate * jax.nn.sigmoid(alpha_glu * gate)).astype(jnp.bfloat16)
        tile = hidden.shape[1]
        for t in range(up_steps):
            lo = t * tile
            hi = min(ff, lo + tile)

            @pl.when(step == t)
            def _():
                h_ref[:, lo:hi] = hidden[:, : hi - lo]

    @pl.when(step >= up_steps)
    def _():
        made = jnp.dot(h_ref[...], down_ref[0], preferred_element_type=jnp.float32)
        made = made.astype(jnp.bfloat16)
        tile = made.shape[1]
        down_steps = -(-width // tile)
        for t in range(down_steps):
            lo = t * tile
            hi = min(width, lo + tile)

            @pl.when(step == up_steps + t)
            def _():
                o_ref[:, lo:hi] = made[:, : hi - lo]

    @pl.when(step == pl.num_programs(0) - 1)
    def _():
        for base, dst in ((0, own_out), (part, far_out)):
            for q in range(fold.groups):
                lo = q * fold.padded
                dst[:, lo : lo + width] = o_ref[base + q * block : base + (q + 1) * block, :]
            at = base + fold.groups * block
            total = None
            for p, lo, hi in fold.spans():
                rows = lax.dot_general(
                    tail_pick(fold, sources, p),
                    o_ref[at : at + sources * fold.rest, lo:hi],
                    (((0,), (0,)), ((), ())),
                    preferred_element_type=jnp.float32,
                )
                if hi - lo < fold.piece:
                    blank = jnp.zeros((rows.shape[0], fold.piece - (hi - lo)), jnp.float32)
                    rows = jnp.concatenate([rows, blank], axis=1)
                total = rows if total is None else total + rows
            if total is not None:
                dst[:, fold.tail_at :] = total.astype(jnp.bfloat16)


def whole_block(shape):
    return pl.BlockSpec(shape, lambda *_: (0,) * len(shape), pipeline_mode=pl.Buffered(1))


def run_experts(fold, sources, own, far, w_gate, w_up, w_down):
    width, ff = w_gate.shape[1], w_gate.shape[2]
    up_tile = min(TILE, ff)
    down_tile = min(TILE, width)
    up_steps = -(-ff // up_tile)
    down_steps = -(-width // down_tile)
    rows = 2 * sources * fold.slots
    up_spec = pl.BlockSpec((1, width, up_tile), lambda i: (0, 0, jnp.minimum(i, up_steps - 1)))
    down_spec = pl.BlockSpec((1, ff, down_tile), lambda i: (0, 0, jnp.maximum(i - up_steps, 0)))
    return pl.pallas_call(
        functools.partial(expert_kernel, fold, sources, up_steps),
        out_shape=(jax.ShapeDtypeStruct(own.shape, own.dtype),) * 2,
        grid=(up_steps + down_steps,),
        in_specs=[whole_block(own.shape), whole_block(far.shape), up_spec, up_spec, down_spec],
        out_specs=(whole_block(own.shape),) * 2,
        scratch_shapes=[
            pltpu.VMEM((rows, width), jnp.bfloat16),
            pltpu.VMEM((rows, ff), jnp.bfloat16),
            pltpu.VMEM((rows, width), jnp.bfloat16),
        ],
        name="experts",
        cost_estimate=pl.CostEstimate(
            flops=6 * rows * width * ff,
            bytes_accessed=6 * width * ff + 8 * own.size,
            transcendentals=rows * ff,
        ),
    )(own, far, w_gate, w_up, w_down)


def body(tokens, expert_ids, route_weights, w_gate, w_up, w_down):
    site_count = lax.axis_size("site")
    members = lax.axis_size("member")
    experts = EXP_SITE * site_count
    split = members // EXP_SITE
    tok_count, width = tokens.shape
    top_count = expert_ids.shape[1]
    mean_rows = tok_count * top_count // experts
    most_rows = mean_rows + max(1, mean_rows // 8)
    half = site_count // 2
    chunks = experts // 2
    sources = half * members
    fold = Fold(most_rows, width)

    swap = [(s, (s + half) % site_count) for s in range(site_count)]
    halves = [list(range(h * sources, (h + 1) * sources)) for h in range(2)]
    first = (lax.axis_index("site") // half * chunks).astype(jnp.float32)

    def exchange(value):
        return lax.all_to_all(
            value, ("site", "member"), split_axis=0, concat_axis=0, tiled=True,
            axis_index_groups=halves,
        )

    def local(route):
        return jnp.concatenate([route[:top_count] - first, route[top_count:]], axis=0)

    def pack(route, rows):
        packed = pl.pallas_call(
            functools.partial(pack_kernel, fold, chunks),
            out_shape=jax.ShapeDtypeStruct((chunks * SUB, fold.total), rows.dtype),
            name="pack",
        )(route, rows)
        if split > 1:
            packed = jnp.repeat(packed.reshape(chunks, SUB, -1), split, axis=0)
            packed = packed.reshape(sources * SUB, -1)
        return packed

    route = jnp.concatenate(
        [expert_ids.T.astype(jnp.float32), route_weights.T.astype(jnp.float32)], axis=0
    )
    far_tokens = lax.ppermute(tokens, "site", swap)
    far_route = local(lax.ppermute(route, "site", swap))
    route = local(route)

    own_in = exchange(pack(route, tokens))
    far_in = exchange(pack(far_route, far_tokens))
    own_made, far_made = run_experts(fold, sources, own_in, far_in, w_gate, w_up, w_down)

    def spread(value):
        if split == 1:
            return value
        value = value.reshape(chunks, split, SUB, -1)
        return jnp.sum(value.astype(jnp.float32), axis=1).astype(value.dtype).reshape(chunks * SUB, -1)

    far_back = spread(exchange(far_made))
    far_sum = pl.pallas_call(
        functools.partial(held_kernel, fold, chunks),
        out_shape=jax.ShapeDtypeStruct(tokens.shape, tokens.dtype),
        name="held",
    )(far_route, far_back)
    own_made, far_sum = lax.optimization_barrier((own_made, far_sum))
    other = lax.ppermute(far_sum, "site", [(b, a) for a, b in swap])
    own_back = spread(exchange(own_made))
    return pl.pallas_call(
        functools.partial(final_kernel, fold, chunks),
        out_shape=jax.ShapeDtypeStruct(tokens.shape, tokens.dtype),
        name="final",
    )(route, own_back, other)


def solution(mesh):
    placed = (
        P(("groups", "site", "member"), None),
        P(("groups", "site", "member"), None),
        P(("groups", "site", "member"), None),
        P(("site", "member"), None, None),
        P(("site", "member"), None, None),
        P(("site", "member"), None, None),
    )
    return jax.shard_map(
        body,
        mesh=mesh,
        in_specs=placed,
        out_specs=P(("groups", "site", "member"), None),
        check_vma=False,
    )
```

```python
import functools

import jax
import jax.numpy as jnp
from jax import lax
from jax.experimental import pallas as pl
from jax.experimental.pallas import tpu as pltpu
from jax.sharding import PartitionSpec as P

EXP_SITE = 4
LANE = 128
SUB = 8
TILE = 512
DEPTH = 3
MOST_PERMUTES = 8
SMALL = 12 << 20
MIDDLE = 44 << 20
LARGE = 60 * 1024 * 1024

alpha_glu = 1.702


class Fold:
    def __init__(self, rows, width):
        self.rows = rows
        self.width = width
        self.padded = -(-width // LANE) * LANE
        self.groups = rows // SUB
        self.rest = rows % SUB
        if self.rest and SUB % self.rest:
            self.groups, self.rest = self.groups + 1, 0
        self.pieces = SUB // self.rest if self.rest else 0
        tiles = self.padded // LANE
        self.piece = -(-tiles // self.pieces) * LANE if self.rest else 0
        self.tail_at = self.groups * self.padded
        self.total = self.tail_at + self.piece
        self.slots = self.groups * SUB + self.rest

    def spans(self):
        for p in range(self.pieces):
            lo = p * self.piece
            hi = min(self.width, lo + self.piece)
            if hi > lo:
                yield p, lo, hi


class Plan:
    def __init__(self, half, members, chunks, fold, ff):
        self.half = half
        self.members = members
        self.chunks = chunks
        self.sources = half * members
        self.split = self.sources // chunks
        self.pairwise = self.sources <= MOST_PERMUTES and self.sources & (self.sources - 1) == 0
        self.fold = fold
        self.ff = ff
        self.parts = self.sources if self.pairwise else 1
        self.part_rows = self.sources * SUB // self.parts

    def expert_of(self, chunk):
        site = lax.axis_index("site")
        if self.pairwise:
            me = site % self.half * self.members + lax.axis_index("member")
            chunk = jnp.bitwise_xor(chunk, me)
        return site // self.half * self.chunks + chunk // self.split

    def gather(self, refs, stage_ref):
        for k, ref in enumerate(refs):
            stage_ref[k * self.part_rows : (k + 1) * self.part_rows, :] = ref[...]

    def scatter(self, stage_ref, refs):
        for k, ref in enumerate(refs):
            ref[...] = stage_ref[k * self.part_rows : (k + 1) * self.part_rows, :]

    @property
    def stage(self):
        return pltpu.VMEM((self.sources * SUB, self.fold.total), jnp.bfloat16)

    @property
    def part_shape(self):
        return jax.ShapeDtypeStruct((self.part_rows, self.fold.total), jnp.bfloat16)


def slot_masks(route, plan):
    fold = plan.fold
    top = route.shape[0] // 2
    tokens = route.shape[1]
    shape = (plan.sources * SUB, tokens)
    row = lax.broadcasted_iota(jnp.int32, shape, 0)
    group = plan.expert_of(row // SUB).astype(jnp.float32)
    sub = row % SUB
    need = jnp.zeros(shape, jnp.float32)
    weight = jnp.zeros(shape, jnp.float32)
    for k in range(top):
        hit = route[k : k + 1, :] == group
        need = jnp.where(hit, 1.0, need)
        weight = jnp.where(hit, route[top + k : top + k + 1, :], weight)
    before = (
        lax.broadcasted_iota(jnp.int32, (tokens, tokens), 0)
        < lax.broadcasted_iota(jnp.int32, (tokens, tokens), 1)
    ).astype(jnp.bfloat16)
    position = jnp.dot(need.astype(jnp.bfloat16), before, preferred_element_type=jnp.float32)
    position = jnp.where(need > 0, position, -1.0)
    subf = sub.astype(jnp.float32)
    mains = [position == subf + float(SUB * q) for q in range(fold.groups)]
    tails = []
    for p in range(fold.pieces):
        slot = (sub // fold.pieces).astype(jnp.float32) + float(SUB * fold.groups)
        tails.append((position == slot) & (sub % fold.pieces == p))
    return mains, tails, weight


def pack_rows(route, plan, tokens_ref, out_ref):
    fold = plan.fold
    mains, tails, _ = slot_masks(route, plan)
    for q, mask in enumerate(mains):
        pick = jnp.where(mask, 1.0, 0.0).astype(jnp.bfloat16)
        rows = jnp.dot(pick, tokens_ref[...], preferred_element_type=jnp.float32)
        lo = q * fold.padded
        out_ref[:, lo : lo + fold.width] = rows.astype(jnp.bfloat16)
    if tails:
        total = None
        for p, lo, hi in fold.spans():
            pick = jnp.where(tails[p], 1.0, 0.0).astype(jnp.bfloat16)
            piece = jnp.dot(pick, tokens_ref[:, lo:hi], preferred_element_type=jnp.float32)
            if hi - lo < fold.piece:
                blank = jnp.zeros((piece.shape[0], fold.piece - (hi - lo)), jnp.float32)
                piece = jnp.concatenate([piece, blank], axis=1)
            total = piece if total is None else total + piece
        out_ref[:, fold.tail_at :] = total.astype(jnp.bfloat16)


def own_pack_kernel(plan, ids_ref, weights_ref, tokens_ref, *refs):
    out_refs, route_ref, stage_ref = refs[:-2], refs[-2], refs[-1]
    top = ids_ref.shape[0]
    route_ref[0:top, :] = ids_ref[...].astype(jnp.float32)
    route_ref[top:, :] = weights_ref[...].astype(jnp.float32)
    pack_rows(route_ref[...], plan, tokens_ref, stage_ref)
    plan.scatter(stage_ref, out_refs)


def far_pack_kernel(plan, route_ref, tokens_ref, *refs):
    out_refs, stage_ref = refs[:-1], refs[-1]
    pack_rows(route_ref[...], plan, tokens_ref, stage_ref)
    plan.scatter(stage_ref, out_refs)


def weighted_sum(plan, route, returned_ref):
    fold = plan.fold
    mains, tails, weight = slot_masks(route, plan)
    contract = (((0,), (0,)), ((), ()))
    total = None
    for q, mask in enumerate(mains):
        scale = jnp.where(mask, weight, 0.0).astype(jnp.bfloat16)
        lo = q * fold.padded
        term = lax.dot_general(
            scale,
            returned_ref[:, lo : lo + fold.width],
            contract,
            preferred_element_type=jnp.float32,
        )
        total = term if total is None else total + term
    if tails:
        pieces = []
        for p, lo, hi in fold.spans():
            scale = jnp.where(tails[p], weight, 0.0).astype(jnp.bfloat16)
            pieces.append(
                lax.dot_general(
                    scale,
                    returned_ref[:, fold.tail_at : fold.tail_at + (hi - lo)],
                    contract,
                    preferred_element_type=jnp.float32,
                )
            )
        term = jnp.concatenate(pieces, axis=1)
        total = term if total is None else total + term
    return total


def held_kernel(plan, route_ref, *refs):
    in_refs, out_ref, stage_ref = refs[:-2], refs[-2], refs[-1]
    plan.gather(in_refs, stage_ref)
    out_ref[...] = weighted_sum(plan, route_ref[...], stage_ref).astype(jnp.bfloat16)


def final_kernel(plan, route_ref, other_ref, *refs):
    in_refs, out_ref, stage_ref = refs[:-2], refs[-2], refs[-1]
    plan.gather(in_refs, stage_ref)
    total = weighted_sum(plan, route_ref[...], stage_ref)
    out_ref[...] = (total + other_ref[...].astype(jnp.float32)).astype(jnp.bfloat16)


def tail_pick(fold, sources, p):
    shape = (sources * fold.rest, sources * SUB)
    row = lax.broadcasted_iota(jnp.int32, shape, 0)
    col = lax.broadcasted_iota(jnp.int32, shape, 1)
    want = (row // fold.rest) * SUB + (row % fold.rest) * fold.pieces + p
    return jnp.where(col == want, 1.0, 0.0).astype(jnp.bfloat16)


def column_tiles(count):
    tiles, at = [], 0
    while count - at >= LANE:
        size = min(TILE // 2 if at < TILE else TILE, (count - at) // LANE * LANE)
        if count - at - size < LANE:
            size = count - at
        tiles.append((at, size))
        at += size
    if at < count:
        tiles.append((at, count - at))
    return tiles


def unfold(plan, src, x_ref):
    fold, block = plan.fold, plan.sources * SUB
    for q in range(fold.groups):
        lo = q * fold.padded
        x_ref[q * block : (q + 1) * block, :] = src[:, lo : lo + fold.width]
    at = fold.groups * block
    for p, lo, hi in fold.spans():
        rows = jnp.dot(
            tail_pick(fold, plan.sources, p),
            src[:, fold.tail_at : fold.tail_at + (hi - lo)],
            preferred_element_type=jnp.float32,
        )
        x_ref[at : at + plan.sources * fold.rest, lo:hi] = rows.astype(jnp.bfloat16)


def refold(plan, o_ref, dst):
    fold, block = plan.fold, plan.sources * SUB
    for q in range(fold.groups):
        lo = q * fold.padded
        dst[:, lo : lo + fold.width] = o_ref[q * block : (q + 1) * block, :]
    at = fold.groups * block
    total = None
    for p, lo, hi in fold.spans():
        rows = lax.dot_general(
            tail_pick(fold, plan.sources, p),
            o_ref[at : at + plan.sources * fold.rest, lo:hi],
            (((0,), (0,)), ((), ())),
            preferred_element_type=jnp.float32,
        )
        if hi - lo < fold.piece:
            blank = jnp.zeros((rows.shape[0], fold.piece - (hi - lo)), jnp.float32)
            rows = jnp.concatenate([rows, blank], axis=1)
        total = rows if total is None else total + rows
    if total is not None:
        dst[:, fold.tail_at :] = total.astype(jnp.bfloat16)


def expert_kernel(plan, up_tiles, down_tiles, *refs):
    refs = list(refs)
    n = plan.parts

    def take(count):
        taken = refs[:count]
        del refs[:count]
        return taken

    if up_tiles:
        in_refs = take(n)
        hbm = take(2)
    else:
        (h_ref,) = take(1)
        hbm = []
    if down_tiles:
        hbm = hbm + take(1)
        out_refs = take(n)
    else:
        (h_ref,) = take(1)
    (stage_ref,) = take(1)
    if up_tiles:
        (x_ref,) = take(1)
    if up_tiles and down_tiles:
        (h_ref,) = take(1)
    if down_tiles:
        (o_ref,) = take(1)
    sems = refs.pop()
    ring, last = refs[: len(hbm)], refs[len(hbm) :]
    down_at = len(hbm) - 1

    def slot(which, tiles, t):
        size = tiles[t][1]
        if t == len(tiles) - 1:
            return last[which]
        ref = ring[which].at[t % DEPTH]
        return ref if size == TILE else ref.at[:, 0:size]

    def copy(which, tiles, t):
        lo, size = tiles[t]
        sem = DEPTH if t == len(tiles) - 1 else t % DEPTH
        return pltpu.make_async_copy(
            hbm[which].at[0, :, lo : lo + size], slot(which, tiles, t), sems.at[which, sem]
        )

    jobs = [[copy(0, up_tiles, t), copy(1, up_tiles, t)] for t in range(len(up_tiles))]
    jobs += [[copy(down_at, down_tiles, t)] for t in range(len(down_tiles))]

    for job in jobs[:DEPTH]:
        for c in job:
            c.start()
    if up_tiles:
        plan.gather(in_refs, stage_ref)
        unfold(plan, stage_ref, x_ref)

    for j, job in enumerate(jobs):
        for c in job:
            c.wait()
        if j < len(up_tiles):
            lo, size = up_tiles[j]
            gate = jnp.dot(x_ref[...], slot(0, up_tiles, j)[...], preferred_element_type=jnp.float32)
            up = jnp.dot(x_ref[...], slot(1, up_tiles, j)[...], preferred_element_type=jnp.float32)
            hidden = (up + 1.0) * gate * jax.nn.sigmoid(alpha_glu * gate)
            h_ref[:, lo : lo + size] = hidden.astype(jnp.bfloat16)
        else:
            t = j - len(up_tiles)
            lo, size = down_tiles[t]
            weights = slot(down_at, down_tiles, t)[...]
            made = jnp.dot(h_ref[...], weights, preferred_element_type=jnp.float32)
            o_ref[:, lo : lo + size] = made.astype(jnp.bfloat16)
        if j + DEPTH < len(jobs):
            for c in jobs[j + DEPTH]:
                c.start()
    if down_tiles:
        refold(plan, o_ref, stage_ref)
        plan.scatter(stage_ref, out_refs)


def vmem_params(limit):
    return pltpu.CompilerParams(vmem_limit_bytes=limit)


def run_experts(plan, rows_in, up_weights, down_weight, limit):
    width, ff = plan.fold.width, plan.ff
    up_tiles = column_tiles(ff) if up_weights else []
    down_tiles = column_tiles(width) if down_weight is not None else []
    rows = plan.sources * plan.fold.slots
    here = pl.BlockSpec(memory_space=pltpu.VMEM)
    there = pl.BlockSpec(memory_space=pltpu.HBM)
    vmem = lambda *shape: pltpu.VMEM(shape, jnp.bfloat16)
    weights = list(up_weights) + ([down_weight] if down_tiles else [])
    if down_tiles:
        out_shape = [plan.part_shape] * plan.parts
    else:
        out_shape = [jax.ShapeDtypeStruct((rows, ff), jnp.bfloat16)]
    scratch = [plan.stage]
    if up_tiles:
        scratch.append(vmem(rows, width))
    if up_tiles and down_tiles:
        scratch.append(vmem(rows, ff))
    if down_tiles:
        scratch.append(vmem(rows, width))
    rings, lasts = [], []
    for tiles, depth in [(up_tiles, width)] * len(up_weights) + [(down_tiles, ff)] * bool(down_tiles):
        rings.append(vmem(DEPTH, depth, TILE))
        lasts.append(vmem(depth, tiles[-1][1]))
    scratch += rings + lasts + [pltpu.SemaphoreType.DMA((len(weights), DEPTH + 1))]
    return pl.pallas_call(
        functools.partial(expert_kernel, plan, up_tiles, down_tiles),
        out_shape=out_shape,
        in_specs=[here] * len(rows_in) + [there] * len(weights),
        out_specs=[here] * len(out_shape),
        scratch_shapes=scratch,
        compiler_params=vmem_params(limit),
        cost_estimate=pl.CostEstimate(
            flops=2 * len(weights) * rows * width * ff,
            bytes_accessed=2 * len(weights) * width * ff,
            transcendentals=rows * ff if up_tiles else 0,
        ),
    )(*rows_in, *weights)


def body(tokens, expert_ids, route_weights, w_gate, w_up, w_down):
    site_count = lax.axis_size("site")
    members = lax.axis_size("member")
    experts = EXP_SITE * site_count
    tok_count, width = tokens.shape
    top_count = expert_ids.shape[1]
    mean_rows = tok_count * top_count // experts
    most_rows = mean_rows + max(1, mean_rows // 8)
    half = site_count // 2
    plan = Plan(half, members, experts // 2, Fold(most_rows, width), w_gate.shape[2])
    sources = plan.sources

    swap = [(s, (s + half) % site_count) for s in range(site_count)]
    halves = [list(range(h * sources, (h + 1) * sources)) for h in range(2)]

    def exchange(parts):
        if not plan.pairwise:
            return [
                lax.all_to_all(
                    parts[0], ("site", "member"), split_axis=0, concat_axis=0, tiled=True,
                    axis_index_groups=halves,
                )
            ]
        return [parts[0]] + [
            lax.ppermute(parts[k], ("site", "member"), [(i, i ^ k) for i in range(2 * sources)])
            for k in range(1, sources)
        ]

    small = vmem_params(SMALL if plan.pairwise else LARGE)
    parts_shape = [plan.part_shape] * plan.parts
    rows_shape = jax.ShapeDtypeStruct(tokens.shape, tokens.dtype)
    route_shape = jax.ShapeDtypeStruct((2 * top_count, tok_count), jnp.float32)

    def call(kernel, out_shape):
        return pl.pallas_call(
            functools.partial(kernel, plan),
            out_shape=out_shape,
            scratch_shapes=[plan.stage],
            compiler_params=small,
        )

    limit = MIDDLE if plan.pairwise else LARGE

    far_tokens = lax.ppermute(tokens, "site", swap)
    *own_packed, route = call(own_pack_kernel, parts_shape + [route_shape])(
        expert_ids.T, route_weights.T, tokens
    )
    far_route = lax.ppermute(route, "site", swap)
    own_in = exchange(own_packed)
    far_packed = call(far_pack_kernel, parts_shape)(far_route, far_tokens)
    far_in = exchange(far_packed)
    own_hidden = run_experts(plan, own_in, (w_gate, w_up), None, limit)
    far_made = run_experts(plan, far_in, (w_gate, w_up), w_down, limit)
    far_back = exchange(far_made)
    own_made = run_experts(plan, own_hidden, (), w_down, limit)
    far_sum = call(held_kernel, rows_shape)(far_route, *far_back)
    other = lax.ppermute(far_sum, "site", [(b, a) for a, b in swap])
    own_back = exchange(own_made)
    return call(final_kernel, rows_shape)(route, other, *own_back)


def solution(mesh):
    placed = (
        P(("groups", "site", "member"), None),
        P(("groups", "site", "member"), None),
        P(("groups", "site", "member"), None),
        P(("site", "member"), None, None),
        P(("site", "member"), None, None),
        P(("site", "member"), None, None),
    )
    return jax.shard_map(
        body,
        mesh=mesh,
        in_specs=placed,
        out_specs=P(("groups", "site", "member"), None),
        check_vma=False,
    )
```

```python
import functools

import jax
import jax.numpy as jnp
from jax import lax
from jax.experimental import pallas as pl
from jax.experimental.pallas import tpu as pltpu
from jax.sharding import PartitionSpec as P

EXP_SITE = 4
LANE = 128
SUB = 8
TILE = 512
DEPTH = 3
MOST_PERMUTES = 8
MIDDLE = 18 << 20
LARGE = 60 * 1024 * 1024

alpha_glu = 1.702


class Fold:
    def __init__(self, rows, width):
        self.rows = rows
        self.width = width
        self.padded = -(-width // LANE) * LANE
        self.groups = rows // SUB
        self.rest = rows % SUB
        if self.rest and SUB % self.rest:
            self.groups, self.rest = self.groups + 1, 0
        self.pieces = SUB // self.rest if self.rest else 0
        tiles = self.padded // LANE
        self.piece = -(-tiles // self.pieces) * LANE if self.rest else 0
        self.tail_at = self.groups * self.padded
        self.total = self.tail_at + self.piece
        self.slots = self.groups * SUB + self.rest

    def spans(self):
        for p in range(self.pieces):
            lo = p * self.piece
            hi = min(self.width, lo + self.piece)
            if hi > lo:
                yield p, lo, hi


class Plan:
    def __init__(self, half, members, chunks, fold, ff):
        self.half = half
        self.members = members
        self.chunks = chunks
        self.sources = half * members
        self.split = self.sources // chunks
        self.pairwise = self.sources <= MOST_PERMUTES and self.sources & (self.sources - 1) == 0
        self.fold = fold
        self.ff = ff
        self.parts = self.sources if self.pairwise else 1
        self.resident = self.pairwise
        self.part_rows = self.sources * SUB // self.parts

    def expert_of(self, chunk):
        site = lax.axis_index("site")
        if self.pairwise:
            me = site % self.half * self.members + lax.axis_index("member")
            chunk = jnp.bitwise_xor(chunk, me)
        return site // self.half * self.chunks + chunk // self.split

    def gather(self, refs, stage_ref):
        for k, ref in enumerate(refs):
            stage_ref[k * self.part_rows : (k + 1) * self.part_rows, :] = ref[...]

    def scatter(self, stage_ref, refs):
        for k, ref in enumerate(refs):
            ref[...] = stage_ref[k * self.part_rows : (k + 1) * self.part_rows, :]

    @property
    def stage(self):
        return pltpu.VMEM((self.sources * SUB, self.fold.total), jnp.bfloat16)

    @property
    def part_shape(self):
        return jax.ShapeDtypeStruct((self.part_rows, self.fold.total), jnp.bfloat16)


def slot_masks(route, plan):
    fold = plan.fold
    top = route.shape[0] // 2
    tokens = route.shape[1]
    shape = (plan.sources * SUB, tokens)
    row = lax.broadcasted_iota(jnp.int32, shape, 0)
    group = plan.expert_of(row // SUB).astype(jnp.float32)
    sub = row % SUB
    need = jnp.zeros(shape, jnp.float32)
    weight = jnp.zeros(shape, jnp.float32)
    for k in range(top):
        hit = route[k : k + 1, :] == group
        need = jnp.where(hit, 1.0, need)
        weight = jnp.where(hit, route[top + k : top + k + 1, :], weight)
    before = (
        lax.broadcasted_iota(jnp.int32, (tokens, tokens), 0)
        < lax.broadcasted_iota(jnp.int32, (tokens, tokens), 1)
    ).astype(jnp.bfloat16)
    position = jnp.dot(need.astype(jnp.bfloat16), before, preferred_element_type=jnp.float32)
    position = jnp.where(need > 0, position, -1.0)
    subf = sub.astype(jnp.float32)
    mains = [position == subf + float(SUB * q) for q in range(fold.groups)]
    tails = []
    for p in range(fold.pieces):
        slot = (sub // fold.pieces).astype(jnp.float32) + float(SUB * fold.groups)
        tails.append((position == slot) & (sub % fold.pieces == p))
    return mains, tails, weight


def pack_rows(route, plan, tokens_ref, out_ref):
    fold = plan.fold
    mains, tails, _ = slot_masks(route, plan)
    for q, mask in enumerate(mains):
        pick = jnp.where(mask, 1.0, 0.0).astype(jnp.bfloat16)
        rows = jnp.dot(pick, tokens_ref[...], preferred_element_type=jnp.float32)
        lo = q * fold.padded
        out_ref[:, lo : lo + fold.width] = rows.astype(jnp.bfloat16)
    if tails:
        total = None
        for p, lo, hi in fold.spans():
            pick = jnp.where(tails[p], 1.0, 0.0).astype(jnp.bfloat16)
            piece = jnp.dot(pick, tokens_ref[:, lo:hi], preferred_element_type=jnp.float32)
            if hi - lo < fold.piece:
                blank = jnp.zeros((piece.shape[0], fold.piece - (hi - lo)), jnp.float32)
                piece = jnp.concatenate([piece, blank], axis=1)
            total = piece if total is None else total + piece
        out_ref[:, fold.tail_at :] = total.astype(jnp.bfloat16)


def own_pack_kernel(plan, ids_ref, weights_ref, tokens_ref, *refs):
    out_refs, route_ref, stage_ref = refs[:-2], refs[-2], refs[-1]
    top = ids_ref.shape[0]
    route_ref[0:top, :] = ids_ref[...].astype(jnp.float32)
    route_ref[top:, :] = weights_ref[...].astype(jnp.float32)
    pack_rows(route_ref[...], plan, tokens_ref, stage_ref)
    plan.scatter(stage_ref, out_refs)


def far_pack_kernel(plan, route_ref, tokens_ref, *refs):
    out_refs, stage_ref = refs[:-1], refs[-1]
    pack_rows(route_ref[...], plan, tokens_ref, stage_ref)
    plan.scatter(stage_ref, out_refs)


def weighted_sum(plan, route, returned_ref):
    fold = plan.fold
    mains, tails, weight = slot_masks(route, plan)
    contract = (((0,), (0,)), ((), ()))
    total = None
    for q, mask in enumerate(mains):
        scale = jnp.where(mask, weight, 0.0).astype(jnp.bfloat16)
        lo = q * fold.padded
        term = lax.dot_general(
            scale,
            returned_ref[:, lo : lo + fold.width],
            contract,
            preferred_element_type=jnp.float32,
        )
        total = term if total is None else total + term
    if tails:
        pieces = []
        for p, lo, hi in fold.spans():
            scale = jnp.where(tails[p], weight, 0.0).astype(jnp.bfloat16)
            pieces.append(
                lax.dot_general(
                    scale,
                    returned_ref[:, fold.tail_at : fold.tail_at + (hi - lo)],
                    contract,
                    preferred_element_type=jnp.float32,
                )
            )
        term = jnp.concatenate(pieces, axis=1)
        total = term if total is None else total + term
    return total


def held_kernel(plan, route_ref, *refs):
    in_refs, out_ref, stage_ref = refs[:-2], refs[-2], refs[-1]
    plan.gather(in_refs, stage_ref)
    out_ref[...] = weighted_sum(plan, route_ref[...], stage_ref).astype(jnp.bfloat16)


def final_kernel(plan, route_ref, other_ref, *refs):
    in_refs, out_ref, stage_ref = refs[:-2], refs[-2], refs[-1]
    plan.gather(in_refs, stage_ref)
    total = weighted_sum(plan, route_ref[...], stage_ref)
    out_ref[...] = (total + other_ref[...].astype(jnp.float32)).astype(jnp.bfloat16)


def tail_pick(fold, sources, p):
    shape = (sources * fold.rest, sources * SUB)
    row = lax.broadcasted_iota(jnp.int32, shape, 0)
    col = lax.broadcasted_iota(jnp.int32, shape, 1)
    want = (row // fold.rest) * SUB + (row % fold.rest) * fold.pieces + p
    return jnp.where(col == want, 1.0, 0.0).astype(jnp.bfloat16)


def column_tiles(count):
    tiles, at = [], 0
    while count - at >= LANE:
        size = min(TILE // 2 if at < TILE else TILE, (count - at) // LANE * LANE)
        if count - at - size < LANE:
            size = count - at
        tiles.append((at, size))
        at += size
    if at < count:
        tiles.append((at, count - at))
    return tiles


def unfold(plan, src, x_ref):
    fold, block = plan.fold, plan.sources * SUB
    for q in range(fold.groups):
        lo = q * fold.padded
        x_ref[q * block : (q + 1) * block, :] = src[:, lo : lo + fold.width]
    at = fold.groups * block
    for p, lo, hi in fold.spans():
        rows = jnp.dot(
            tail_pick(fold, plan.sources, p),
            src[:, fold.tail_at : fold.tail_at + (hi - lo)],
            preferred_element_type=jnp.float32,
        )
        x_ref[at : at + plan.sources * fold.rest, lo:hi] = rows.astype(jnp.bfloat16)


def refold(plan, o_ref, dst):
    fold, block = plan.fold, plan.sources * SUB
    for q in range(fold.groups):
        lo = q * fold.padded
        dst[:, lo : lo + fold.width] = o_ref[q * block : (q + 1) * block, :]
    at = fold.groups * block
    total = None
    for p, lo, hi in fold.spans():
        rows = lax.dot_general(
            tail_pick(fold, plan.sources, p),
            o_ref[at : at + plan.sources * fold.rest, lo:hi],
            (((0,), (0,)), ((), ())),
            preferred_element_type=jnp.float32,
        )
        if hi - lo < fold.piece:
            blank = jnp.zeros((rows.shape[0], fold.piece - (hi - lo)), jnp.float32)
            rows = jnp.concatenate([rows, blank], axis=1)
        total = rows if total is None else total + rows
    if total is not None:
        dst[:, fold.tail_at :] = total.astype(jnp.bfloat16)


def expert_kernel(plan, up_tiles, down_tiles, *refs):
    refs = list(refs)
    n = plan.parts

    def take(count):
        taken = refs[:count]
        del refs[:count]
        return taken

    hbm, resident = [], []
    if up_tiles:
        in_refs = take(n)
        if plan.resident:
            resident = [take(len(up_tiles)), take(len(up_tiles))]
        else:
            hbm = take(2)
    else:
        (h_ref,) = take(1)
    if down_tiles:
        hbm = hbm + take(1)
        out_refs = take(n)
    else:
        (h_ref,) = take(1)
    (stage_ref,) = take(1)
    if up_tiles:
        (x_ref,) = take(1)
    if up_tiles and down_tiles:
        (h_ref,) = take(1)
    if down_tiles:
        (o_ref,) = take(1)
    sems = refs.pop() if hbm else None
    ring, last = refs[: len(hbm)], refs[len(hbm) :]
    down_at = len(hbm) - 1
    ahead = len(up_tiles) + DEPTH if resident else DEPTH

    def slot(which, tiles, t):
        size = tiles[t][1]
        if t == len(tiles) - 1:
            return last[which]
        ref = ring[which].at[t % DEPTH]
        return ref if size == TILE else ref.at[:, 0:size]

    def copy(which, tiles, t):
        lo, size = tiles[t]
        sem = DEPTH if t == len(tiles) - 1 else t % DEPTH
        return pltpu.make_async_copy(
            hbm[which].at[0, :, lo : lo + size], slot(which, tiles, t), sems.at[which, sem]
        )

    jobs = [
        [] if resident else [copy(0, up_tiles, t), copy(1, up_tiles, t)]
        for t in range(len(up_tiles))
    ]
    jobs += [[copy(down_at, down_tiles, t)] for t in range(len(down_tiles))]

    for job in jobs[:ahead]:
        for c in job:
            c.start()
    if up_tiles:
        plan.gather(in_refs, stage_ref)
        unfold(plan, stage_ref, x_ref)

    for j, job in enumerate(jobs):
        for c in job:
            c.wait()
        if j < len(up_tiles):
            lo, size = up_tiles[j]
            pair = [m[j] for m in resident] or [slot(0, up_tiles, j), slot(1, up_tiles, j)]
            gate = jnp.dot(x_ref[...], pair[0][...], preferred_element_type=jnp.float32)
            up = jnp.dot(x_ref[...], pair[1][...], preferred_element_type=jnp.float32)
            hidden = (up + 1.0) * gate * jax.nn.sigmoid(alpha_glu * gate)
            h_ref[:, lo : lo + size] = hidden.astype(jnp.bfloat16)
        else:
            t = j - len(up_tiles)
            lo, size = down_tiles[t]
            weights = slot(down_at, down_tiles, t)[...]
            made = jnp.dot(h_ref[...], weights, preferred_element_type=jnp.float32)
            o_ref[:, lo : lo + size] = made.astype(jnp.bfloat16)
        if not resident or j >= len(up_tiles):
            for c in jobs[j + DEPTH] if j + DEPTH < len(jobs) else []:
                c.start()
    if down_tiles:
        refold(plan, o_ref, stage_ref)
        plan.scatter(stage_ref, out_refs)


def load_kernel(tiles, count, *refs):
    hbm, held, sems = refs[:count], refs[count:-1], refs[-1]
    copies = [
        pltpu.make_async_copy(
            ref.at[0, :, lo : lo + size], held[m * len(tiles) + t], sems.at[m, t]
        )
        for t, (lo, size) in enumerate(tiles)
        for m, ref in enumerate(hbm)
    ]
    for c in copies:
        c.start()
    for c in copies:
        c.wait()


def load_weights(weights):
    depth = weights[0].shape[1]
    tiles = column_tiles(weights[0].shape[2])
    return pl.pallas_call(
        functools.partial(load_kernel, tiles, len(weights)),
        out_shape=[pltpu.VMEM((depth, size), jnp.bfloat16) for _ in weights for _, size in tiles],
        in_specs=[pl.BlockSpec(memory_space=pltpu.HBM)] * len(weights),
        out_specs=[pl.BlockSpec(memory_space=pltpu.VMEM)] * (len(weights) * len(tiles)),
        scratch_shapes=[pltpu.SemaphoreType.DMA((len(weights), len(tiles)))],
        name="load",
        compiler_params=vmem_params(MIDDLE),
        cost_estimate=pl.CostEstimate(
            flops=0, bytes_accessed=2 * sum(w.size for w in weights), transcendentals=0
        ),
    )(*[pltpu.with_memory_space_constraint(w, pltpu.HBM) for w in weights])


def vmem_params(limit):
    return pltpu.CompilerParams(vmem_limit_bytes=limit)


def run_experts(plan, rows_in, up_weights, down_weight, limit):
    width, ff = plan.fold.width, plan.ff
    up_tiles = column_tiles(ff) if up_weights else []
    down_tiles = column_tiles(width) if down_weight is not None else []
    rows = plan.sources * plan.fold.slots
    here = pl.BlockSpec(memory_space=pltpu.VMEM)
    there = pl.BlockSpec(memory_space=pltpu.HBM)
    vmem = lambda *shape: pltpu.VMEM(shape, jnp.bfloat16)
    held = list(up_weights) if plan.resident else []
    streamed = [] if plan.resident else list(up_weights)
    weights = streamed + ([down_weight] if down_tiles else [])
    if down_tiles:
        out_shape = [plan.part_shape] * plan.parts
    else:
        out_shape = [jax.ShapeDtypeStruct((rows, ff), jnp.bfloat16)]
    scratch = [plan.stage]
    if up_tiles:
        scratch.append(vmem(rows, width))
    if up_tiles and down_tiles:
        scratch.append(vmem(rows, ff))
    if down_tiles:
        scratch.append(vmem(rows, width))
    rings, lasts = [], []
    for tiles, depth in [(up_tiles, width)] * len(streamed) + [(down_tiles, ff)] * bool(down_tiles):
        rings.append(vmem(DEPTH, depth, TILE))
        lasts.append(vmem(depth, tiles[-1][1]))
    scratch += rings + lasts
    if weights:
        scratch.append(pltpu.SemaphoreType.DMA((len(weights), DEPTH + 1)))
    products = (2 if up_tiles else 0) + (1 if down_tiles else 0)
    return pl.pallas_call(
        functools.partial(expert_kernel, plan, up_tiles, down_tiles),
        out_shape=out_shape,
        in_specs=[here] * (len(rows_in) + len(held)) + [there] * len(weights),
        out_specs=[here] * len(out_shape),
        scratch_shapes=scratch,
        compiler_params=vmem_params(limit),
        cost_estimate=pl.CostEstimate(
            flops=2 * products * rows * width * ff,
            bytes_accessed=2 * products * width * ff,
            transcendentals=rows * ff if up_tiles else 0,
        ),
    )(*rows_in, *held, *[pltpu.with_memory_space_constraint(w, pltpu.HBM) for w in weights])


def body(tokens, expert_ids, route_weights, w_gate, w_up, w_down):
    site_count = lax.axis_size("site")
    members = lax.axis_size("member")
    experts = EXP_SITE * site_count
    tok_count, width = tokens.shape
    top_count = expert_ids.shape[1]
    mean_rows = tok_count * top_count // experts
    most_rows = mean_rows + max(1, mean_rows // 8)
    half = site_count // 2
    plan = Plan(half, members, experts // 2, Fold(most_rows, width), w_gate.shape[2])
    sources = plan.sources

    swap = [(s, (s + half) % site_count) for s in range(site_count)]
    halves = [list(range(h * sources, (h + 1) * sources)) for h in range(2)]

    def exchange(parts):
        if not plan.pairwise:
            return [
                lax.all_to_all(
                    parts[0], ("site", "member"), split_axis=0, concat_axis=0, tiled=True,
                    axis_index_groups=halves,
                )
            ]
        return [parts[0]] + [
            lax.ppermute(parts[k], ("site", "member"), [(i, i ^ k) for i in range(2 * sources)])
            for k in range(1, sources)
        ]

    small = vmem_params(MIDDLE if plan.pairwise else LARGE)
    parts_shape = [plan.part_shape] * plan.parts
    rows_shape = jax.ShapeDtypeStruct(tokens.shape, tokens.dtype)
    route_shape = jax.ShapeDtypeStruct((2 * top_count, tok_count), jnp.float32)

    def call(kernel, out_shape):
        return pl.pallas_call(
            functools.partial(kernel, plan),
            out_shape=out_shape,
            scratch_shapes=[plan.stage],
            compiler_params=small,
        )

    limit = MIDDLE if plan.pairwise else LARGE

    far_tokens = lax.ppermute(tokens, "site", swap)
    *own_packed, route = call(own_pack_kernel, parts_shape + [route_shape])(
        expert_ids.T, route_weights.T, tokens
    )
    far_route = lax.ppermute(route, "site", swap)
    own_in = exchange(own_packed)
    up_weights = load_weights((w_gate, w_up)) if plan.resident else (w_gate, w_up)
    far_packed = call(far_pack_kernel, parts_shape)(far_route, far_tokens)
    far_in = exchange(far_packed)
    own_hidden = run_experts(plan, own_in, up_weights, None, limit)
    far_made = run_experts(plan, far_in, up_weights, w_down, limit)
    far_back = exchange(far_made)
    own_made = run_experts(plan, own_hidden, (), w_down, limit)
    far_sum = call(held_kernel, rows_shape)(far_route, *far_back)
    other = lax.ppermute(far_sum, "site", [(b, a) for a, b in swap])
    own_back = exchange(own_made)
    return call(final_kernel, rows_shape)(route, other, *own_back)


def solution(mesh):
    placed = (
        P(("groups", "site", "member"), None),
        P(("groups", "site", "member"), None),
        P(("groups", "site", "member"), None),
        P(("site", "member"), None, None),
        P(("site", "member"), None, None),
        P(("site", "member"), None, None),
    )
    return jax.shard_map(
        body,
        mesh=mesh,
        in_specs=placed,
        out_specs=P(("groups", "site", "member"), None),
        check_vma=False,
    )
```
